32 devices in a mesh: ctx: 8 (over z, y), wsh: 4 (over x, core).
Axes of the slice: x: 2, y: 2, z: 4, core: 2. Of those that a mesh axis runs over, the one named last changes fastest.
Arguments:
- tokens: bfloat16 [4096, 1024], P(('ctx', 'wsh')), may hold values from -6 to 6
- block_order: int32 [32], replicated, may hold values from 0 to 31, as said below
- segment_ids: int32 [4096], replicated, may hold values from 0 to 7, never falling along the last dimension, each value on 1 to 1024 neighbouring positions
- attn_gain: float32 [1024], replicated, may hold values from 0.5 to 1.5
- query_weight: bfloat16 [1024, 1024], P('wsh'), may hold values from -0.1875 to 0.1875
- key_matrix: bfloat16 [1024, 512], P('wsh'), may hold values from -0.1875 to 0.1875
- value_matrix: bfloat16 [1024, 512], P('wsh'), may hold values from -0.1875 to 0.1875
- query_key_gain: float32 [128], replicated, may hold values from 0.1 to 1.9
- out_weight: bfloat16 [1024, 1024], P('wsh'), may hold values from -1.5 to 1.5
- mlp_gain: float32 [1024], replicated, may hold values from 0.5 to 1.5
- gate_weight: bfloat16 [1024, 4608], P('wsh'), may hold values from -0.1875 to 0.1875
- up_weight: bfloat16 [1024, 4608], P('wsh'), may hold values from -0.1875 to 0.1875
- down_weight: bfloat16 [4608, 1024], P('wsh'), may hold values from -0.09375 to 0.09375
- cotangent: bfloat16 [4096, 1024], P(('ctx', 'wsh')), may hold values from -6 to 6
Outputs:
- output: bfloat16 [4096, 1024], P(('ctx', 'wsh'))
- tokens_grad: float32 [4096, 1024], P(('ctx', 'wsh'))
- query_grad: float32 [1024, 1024], P(('ctx', 'wsh'))
- key_grad: float32 [1024, 512], P(('ctx', 'wsh'))
- value_grad: float32 [1024, 512], P(('ctx', 'wsh'))
- out_grad: float32 [1024, 1024], P(('ctx', 'wsh'))
- gate_grad: float32 [1024, 4608], P(('ctx', 'wsh'))
- up_grad: float32 [1024, 4608], P(('ctx', 'wsh'))
- down_grad: float32 [4608, 1024], P(('ctx', 'wsh'))
- attn_gain_grad: float32 [1024], P(('ctx', 'wsh'))
- qk_gain_grad: float32 [128], P(('ctx', 'wsh'))
- mlp_gain_grad: float32 [1024], P(('ctx', 'wsh'))
The draws below stay inside these ranges and needn't reach their ends.
Inputs may be any that keep to these rules, and one draw needn't show every extreme that they name: `block_order`: A permutation of the blocks. Dealt blocks 2 * 2 * c to 2 * 2 * c + 1 of each ctx index c are blocks of the first sequence (below 16), the next 2 of the second; they stand in pairs at even and odd dealt indices, a block b of a sequence beside block 15 - b of the same sequence. `segment_ids`: never falls along the initial token order; each document holds at most 1024 tokens.
All inputs are finite; a program needn't handle non-finite values.
Results may differ from the reference program's by a relative error of at most 0.033.
Values may be sent and summed in bfloat16 or wider, within the bound.
No kernel may reach another device: no remote copies, remote signals or barrier semaphores. Data moves between devices by JAX's collectives and lax.ppermute only.
A program may use at most 256 MiB of HBM per device.

```python
import math
import jax
import jax.numpy as jnp
import numpy as np
from jax import lax

MODEL_WIDTH = 1024
QUERY_HEAD_COUNT = 16
KEY_VALUE_HEADS = 8
HEAD_SIZE = 64
FF = 4608
BLK = 128
SEQUENCE_COUNT = 2
PAIRS = 1
BLOCKS_SEQ = 16
SEQUENCE_TOKENS = 2048
TOKEN_TOTAL = 4096


def draw_block_order(key, part):
    pair_total = BLOCKS_SEQ // 2
    holders = BLOCKS_SEQ // (2 * PAIRS)
    first_perm = jax.random.permutation(jax.random.fold_in(key, 11), pair_total)
    second_perm = jax.random.permutation(jax.random.fold_in(key, 12), pair_total)
    chosen = jnp.stack([first_perm, second_perm]).reshape(SEQUENCE_COUNT, holders, PAIRS).transpose(1, 0, 2).astype(jnp.int32)
    flipped = jax.random.randint(jax.random.fold_in(key, 13), (holders, SEQUENCE_COUNT, PAIRS), 0, 2)
    mirror = BLOCKS_SEQ - 1 - chosen
    leading = jnp.where(flipped == 0, chosen, mirror)
    trailing = jnp.where(flipped == 0, mirror, chosen)
    paired = jnp.stack([leading, trailing], axis=-1)
    offsets = (jnp.arange(SEQUENCE_COUNT, dtype=jnp.int32) * BLOCKS_SEQ)[None, :, None, None]
    return (paired + offsets).reshape(-1).astype(jnp.int32)


def level_of(stream_key, extent, split, smallest, largest):
    factor_of, own = 1.0, jax.random.fold_in(stream_key, 6)
    for position, blocks in split:
        steps = jnp.exp(jax.random.uniform(jax.random.fold_in(own, position), (blocks,), jnp.float32, smallest / len(split), largest / len(split)))
        factor_of = factor_of * jnp.repeat(steps, extent[position] // blocks).reshape([-1 if axis == position else 1 for axis in range(len(extent))])
    return factor_of


def length_profile(count, total, limit, slope):
    portions = [(1 << 20) // math.isqrt(standing ** slope) + 1 for standing in range(2, count + 1)]
    rest, counts = total - limit - (count - 1), [1] * (count - 1)
    while rest > 0:
        candidates = [i for i in range(count - 1) if counts[i] < limit]
        mass, budget = sum([portions[i] for i in candidates]), rest
        for i in candidates:
            more = min(limit - counts[i], max(1, budget * portions[i] // mass), rest)
            counts[i] = counts[i] + more
            rest = rest - more
    return np.array([limit] + counts)


def uneven_parts(own_key, count, total, limit, skew):
    if count == 2:
        one = jax.random.randint(own_key, (), max(1, total - limit), min(limit, total - 1) + 1)
        return jnp.stack([one, total - one])
    sizes = jnp.asarray(length_profile(count, total, limit, skew), jnp.int32)
    couples = (count - 1) // 2
    donor, taker = sizes[1:1 + 2 * couples:2], sizes[2:2 + 2 * couples:2]
    margin = jnp.minimum(donor - 1, limit - taker)
    shifted = jax.random.randint(jax.random.fold_in(own_key, 1), (couples,), 0, 1 << 20) % (margin + 1)
    sizes = sizes.at[1:1 + 2 * couples:2].set(donor - shifted).at[2:2 + 2 * couples:2].set(taker + shifted)
    return sizes[jax.random.permutation(jax.random.fold_in(own_key, 2), count)]


def centred(key, extent, deviation, reach, pieces=(), held_as=jnp.bfloat16):
    values = deviation * jax.random.normal(key, extent, jnp.float32)
    if pieces:
        values = values * level_of(key, extent, pieces, -0.22, 0.18)
    return jnp.clip(values, -reach, reach).astype(held_as)


def setup_inputs(seed: int = 0) -> dict:
    arg_keys = jax.random.split(jax.random.key(seed), 15)
    return {
        "tokens": centred(arg_keys[0], (TOKEN_TOTAL, MODEL_WIDTH), 1.0, 6.0, ((0, 32),)),
        "block_order": draw_block_order(jax.random.fold_in(arg_keys[14], 71), 0),
        "segment_ids": jnp.searchsorted(jnp.cumsum(uneven_parts(arg_keys[2], 8, TOKEN_TOTAL, SEQUENCE_TOKENS // 2, 1)), jnp.arange(TOKEN_TOTAL), side="right").astype(jnp.int32),
        "attn_gain": jnp.clip(1.0 + 0.1 * jax.random.normal(arg_keys[3], (MODEL_WIDTH,), jnp.float32), 0.5, 1.5),
        "query_weight": centred(arg_keys[4], (MODEL_WIDTH, QUERY_HEAD_COUNT * HEAD_SIZE), MODEL_WIDTH ** -0.5, 0.1875, ((0, 4),)),
        "key_matrix": centred(arg_keys[5], (MODEL_WIDTH, KEY_VALUE_HEADS * HEAD_SIZE), MODEL_WIDTH ** -0.5, 0.1875, ((0, 4),)),
        "value_matrix": centred(arg_keys[6], (MODEL_WIDTH, KEY_VALUE_HEADS * HEAD_SIZE), MODEL_WIDTH ** -0.5, 0.1875, ((0, 4),)),
        "query_key_gain": jnp.clip(1.0 + 0.18 * jax.random.normal(arg_keys[7], (2 * HEAD_SIZE,), jnp.float32), 0.1, 1.9),
        "out_weight": centred(arg_keys[8], (QUERY_HEAD_COUNT * HEAD_SIZE, MODEL_WIDTH), (QUERY_HEAD_COUNT * HEAD_SIZE // 64) ** -0.5, 1.5, ((0, 4),)),
        "mlp_gain": jnp.clip(1.0 + 0.1 * jax.random.normal(arg_keys[9], (MODEL_WIDTH,), jnp.float32), 0.5, 1.5),
        "gate_weight": centred(arg_keys[10], (MODEL_WIDTH, FF), MODEL_WIDTH ** -0.5, 0.1875, ((0, 4),)),
        "up_weight": centred(arg_keys[11], (MODEL_WIDTH, FF), MODEL_WIDTH ** -0.5, 0.1875, ((0, 4),)),
        "down_weight": centred(arg_keys[12], (FF, MODEL_WIDTH), FF ** -0.5, 0.09375, ((0, 4),)),
        "cotangent": centred(arg_keys[13], (TOKEN_TOTAL, MODEL_WIDTH), 1.0, 6.0, ((0, 32),)),
    }


eps_norm = 1e-05
rope_base = 1000000.0

def rms_forward(values, gain_vec):
    norm_scale = lax.rsqrt(lax.optimization_barrier(jnp.mean(values * values, axis=-1, keepdims=True)) + eps_norm)
    normed = values * norm_scale
    return (normed, norm_scale, normed * gain_vec)

def root_mean_square_backward(grad_out, normed, norm_scale, gain_vec):
    grad_normed = grad_out * gain_vec
    inner_term = lax.optimization_barrier(jnp.mean(grad_normed * normed, axis=-1, keepdims=True))
    return norm_scale * (grad_normed - normed * inner_term)

def rope_tables(positions, head_width):
    half_width = head_width // 2
    frequency = rope_base ** (-(jnp.arange(half_width, dtype=jnp.float32) * 2.0) / head_width)
    angles = positions.astype(jnp.float32)[:, None] * frequency[None, :]
    return (jnp.cos(angles), jnp.sin(angles))

def apply_rotary(values, cosine_table, sine_table, direction):
    half_width = values.shape[-1] // 2
    first_half = values[..., :half_width]
    second_half = values[..., half_width:]
    cos_part = cosine_table[:, None, :]
    sin_part = sine_table[:, None, :] * direction
    return jnp.concatenate([first_half * cos_part - second_half * sin_part, second_half * cos_part + first_half * sin_part], axis=-1)

def block_scores(query_block, keys, id_block, seg_block, key_document_index, key_segment_labels):
    scores = jnp.einsum('qgrd,kgd->grqk', query_block.astype(jnp.float32), keys.astype(jnp.float32)) * HEAD_SIZE ** (-0.5)
    allowed = (key_segment_labels[None, :] == seg_block[:, None]) & (key_document_index[None, :] <= id_block[:, None])
    return (scores, allowed[None, None])

def reference(tokens, block_order, segment_ids, attn_gain, query_weight, key_matrix, value_matrix, query_key_gain, out_weight, mlp_gain, gate_weight, up_weight, down_weight, cotangent):
    repeat_heads = QUERY_HEAD_COUNT // KEY_VALUE_HEADS
    rows_per_block = math.gcd(SEQUENCE_TOKENS, 256)
    block_number = SEQUENCE_TOKENS // rows_per_block
    inverse = jnp.argsort(block_order).astype(jnp.int32)

    def to_orig(array):
        return array.reshape((-1, BLK) + array.shape[1:])[inverse].reshape(array.shape)

    def to_dealt(array):
        return array.reshape((-1, BLK) + array.shape[1:])[block_order].reshape(array.shape)
    token_ids = jnp.arange(TOKEN_TOTAL, dtype=jnp.int32)
    positions = token_ids % SEQUENCE_TOKENS
    cosine_table, sine_table = rope_tables(positions, HEAD_SIZE)
    inputs = to_orig(tokens).astype(jnp.float32)
    targets = to_orig(cotangent)
    normed_one, scale_one, pre_one = rms_forward(inputs, attn_gain)
    first_hidden_state = pre_one.astype(jnp.bfloat16)
    query_pre = jnp.dot(first_hidden_state, query_weight, preferred_element_type=jnp.float32).reshape(TOKEN_TOTAL, QUERY_HEAD_COUNT, HEAD_SIZE)
    key_before_norm = jnp.dot(first_hidden_state, key_matrix, preferred_element_type=jnp.float32).reshape(TOKEN_TOTAL, KEY_VALUE_HEADS, HEAD_SIZE)
    value_reduced_precision = jnp.dot(first_hidden_state, value_matrix, preferred_element_type=jnp.float32).astype(jnp.bfloat16)
    query_hat, query_scale, query_normed = rms_forward(query_pre, query_key_gain[:HEAD_SIZE])
    key_unit_normed, key_norm_scale, key_normed = rms_forward(key_before_norm, query_key_gain[HEAD_SIZE:])
    query_rotary = apply_rotary(query_normed, cosine_table, sine_table, 1.0).astype(jnp.bfloat16)
    key_rotary = apply_rotary(key_normed, cosine_table, sine_table, 1.0).astype(jnp.bfloat16)
    query_complete = query_rotary.reshape(SEQUENCE_COUNT, SEQUENCE_TOKENS, KEY_VALUE_HEADS, repeat_heads, HEAD_SIZE)
    key_complete = key_rotary.reshape(SEQUENCE_COUNT, SEQUENCE_TOKENS, KEY_VALUE_HEADS, HEAD_SIZE)
    value_complete = value_reduced_precision.reshape(SEQUENCE_COUNT, SEQUENCE_TOKENS, KEY_VALUE_HEADS, HEAD_SIZE)
    ids_all = token_ids.reshape(SEQUENCE_COUNT, SEQUENCE_TOKENS)
    segs_all = segment_ids.reshape(SEQUENCE_COUNT, SEQUENCE_TOKENS)

    def forward_seq(seq_args):
        query_rows, keys, values, key_document_index, key_segment_labels = seq_args

        def single_block(block_in):
            query_block, id_block, seg_block = block_in
            scores, allowed = block_scores(query_block, keys, id_block, seg_block, key_document_index, key_segment_labels)
            masked = jnp.where(allowed, scores, -1e+30)
            row_max = lax.optimization_barrier(jnp.max(masked, axis=-1))
            row_total = lax.optimization_barrier(jnp.sum(jnp.where(allowed, jnp.exp(masked - row_max[..., None]), 0.0), axis=-1))
            log_total = row_max + jnp.log(row_total)
            prob_low = jnp.where(allowed, jnp.exp(scores - log_total[..., None]), 0.0).astype(jnp.bfloat16)
            attended = jnp.einsum('grqk,kgd->qgrd', prob_low.astype(jnp.float32), values.astype(jnp.float32))
            return (attended.astype(jnp.bfloat16), log_total)
        return lax.map(single_block, (query_rows.reshape(block_number, rows_per_block, KEY_VALUE_HEADS, repeat_heads, HEAD_SIZE), key_document_index.reshape(block_number, rows_per_block), key_segment_labels.reshape(block_number, rows_per_block)))
    attended_all, lse_all = lax.map(forward_seq, (query_complete, key_complete, value_complete, ids_all, segs_all))
    attn_flat = attended_all.reshape(TOKEN_TOTAL, QUERY_HEAD_COUNT * HEAD_SIZE)
    token_block = math.gcd(TOKEN_TOTAL, 4096)
    token_count = TOKEN_TOTAL // token_block

    def mlp_step(state_now, block_in):
        out_acc, gate_acc, up_acc, down_acc, gain_acc = state_now
        input_block, attn_block, target_block = block_in
        mixed = input_block + jnp.dot(attn_block, out_weight, preferred_element_type=jnp.float32)
        normed_two, scale_two, pre_two = rms_forward(mixed, mlp_gain)
        hidden_two = pre_two.astype(jnp.bfloat16)
        gate_pre = jnp.dot(hidden_two, gate_weight, preferred_element_type=jnp.float32)
        up_pre = jnp.dot(hidden_two, up_weight, preferred_element_type=jnp.float32)
        sigmoid_gate = jax.nn.sigmoid(gate_pre)
        swished = gate_pre * sigmoid_gate
        inner_low = (swished * up_pre).astype(jnp.bfloat16)
        result = (mixed + jnp.dot(inner_low, down_weight, preferred_element_type=jnp.float32)).astype(jnp.bfloat16)
        down_acc = down_acc + jnp.dot(inner_low.T, target_block, preferred_element_type=jnp.float32)
        grad_inner = jnp.dot(target_block, down_weight.T, preferred_element_type=jnp.float32)
        gate_low = (grad_inner * up_pre * sigmoid_gate * (1.0 + gate_pre * (1.0 - sigmoid_gate))).astype(jnp.bfloat16)
        up_low = (grad_inner * swished).astype(jnp.bfloat16)
        gate_acc = gate_acc + jnp.dot(hidden_two.T, gate_low, preferred_element_type=jnp.float32)
        up_acc = up_acc + jnp.dot(hidden_two.T, up_low, preferred_element_type=jnp.float32)
        grad_two = jnp.dot(gate_low, gate_weight.T, preferred_element_type=jnp.float32) + jnp.dot(up_low, up_weight.T, preferred_element_type=jnp.float32)
        gain_acc = gain_acc + lax.optimization_barrier(jnp.sum(grad_two * normed_two, axis=0))
        grad_mixed = target_block.astype(jnp.float32) + root_mean_square_backward(grad_two, normed_two, scale_two, mlp_gain)
        mixed_low = grad_mixed.astype(jnp.bfloat16)
        out_acc = out_acc + jnp.dot(attn_block.T, mixed_low, preferred_element_type=jnp.float32)
        grad_attn = jnp.dot(mixed_low, out_weight.T, preferred_element_type=jnp.float32).astype(jnp.bfloat16)
        return ((out_acc, gate_acc, up_acc, down_acc, gain_acc), (result, grad_mixed, grad_attn))
    start_state = (jnp.zeros((QUERY_HEAD_COUNT * HEAD_SIZE, MODEL_WIDTH), jnp.float32), jnp.zeros((MODEL_WIDTH, FF), jnp.float32), jnp.zeros((MODEL_WIDTH, FF), jnp.float32), jnp.zeros((FF, MODEL_WIDTH), jnp.float32), jnp.zeros((MODEL_WIDTH,), jnp.float32))
    mlp_state, feedforward_outputs = lax.scan(mlp_step, start_state, (inputs.reshape(token_count, token_block, MODEL_WIDTH), attn_flat.reshape(token_count, token_block, QUERY_HEAD_COUNT * HEAD_SIZE), targets.reshape(token_count, token_block, MODEL_WIDTH)))
    out_grad, gate_grad, up_grad, down_grad, mlp_gain_grad = mlp_state
    result_all = feedforward_outputs[0].reshape(TOKEN_TOTAL, MODEL_WIDTH)
    grad_mixed_all = feedforward_outputs[1].reshape(TOKEN_TOTAL, MODEL_WIDTH)
    attention_gradient_full = feedforward_outputs[2].reshape(SEQUENCE_COUNT, SEQUENCE_TOKENS, KEY_VALUE_HEADS, repeat_heads, HEAD_SIZE)

    def backward_seq(seq_args):
        query_rows, keys, values, attended_sequence, output_gradient_sequence, logsumexp_sequence, key_document_index, key_segment_labels = seq_args

        def backward_step(state_now, block_in):
            key_acc, value_acc = state_now
            query_block, out_block, dout_block, lse_block, id_block, seg_block = block_in
            scores, allowed = block_scores(query_block, keys, id_block, seg_block, key_document_index, key_segment_labels)
            prob_full = jnp.where(allowed, jnp.exp(scores - lse_block[..., None]), 0.0)
            prob_low = prob_full.astype(jnp.bfloat16)
            value_acc = value_acc + jnp.einsum('grqk,qgrd->kgd', prob_low.astype(jnp.float32), dout_block.astype(jnp.float32))
            grad_prob = jnp.einsum('qgrd,kgd->grqk', dout_block.astype(jnp.float32), values.astype(jnp.float32))
            row_delta = lax.optimization_barrier(jnp.sum(dout_block.astype(jnp.float32) * out_block.astype(jnp.float32), axis=-1)).transpose(1, 2, 0)
            score_low = (prob_full * (grad_prob - row_delta[..., None]) * HEAD_SIZE ** (-0.5)).astype(jnp.bfloat16)
            grad_query = jnp.einsum('grqk,kgd->qgrd', score_low.astype(jnp.float32), keys.astype(jnp.float32))
            key_acc = key_acc + jnp.einsum('grqk,qgrd->kgd', score_low.astype(jnp.float32), query_block.astype(jnp.float32))
            return ((key_acc, value_acc), grad_query)
        keys_zeroed = jnp.zeros((SEQUENCE_TOKENS, KEY_VALUE_HEADS, HEAD_SIZE), jnp.float32)
        output_sums, query_rows_gradient = lax.scan(backward_step, (keys_zeroed, keys_zeroed), (query_rows.reshape(block_number, rows_per_block, KEY_VALUE_HEADS, repeat_heads, HEAD_SIZE), attended_sequence, output_gradient_sequence.reshape(block_number, rows_per_block, KEY_VALUE_HEADS, repeat_heads, HEAD_SIZE), logsumexp_sequence, key_document_index.reshape(block_number, rows_per_block), key_segment_labels.reshape(block_number, rows_per_block)))
        return (query_rows_gradient, output_sums[0], output_sums[1])
    grad_q_all, key_gradient_full, value_gradient_full = lax.map(backward_seq, (query_complete, key_complete, value_complete, attended_all, attention_gradient_full, lse_all, ids_all, segs_all))
    grad_qrot = grad_q_all.reshape(TOKEN_TOTAL, QUERY_HEAD_COUNT, HEAD_SIZE)
    key_rotated_gradient = key_gradient_full.reshape(TOKEN_TOTAL, KEY_VALUE_HEADS, HEAD_SIZE)
    gradient_of_value = value_gradient_full.reshape(TOKEN_TOTAL, KEY_VALUE_HEADS * HEAD_SIZE).astype(jnp.bfloat16)
    grad_qn = apply_rotary(grad_qrot, cosine_table, sine_table, -1.0)
    key_normed_gradient = apply_rotary(key_rotated_gradient, cosine_table, sine_table, -1.0)
    qk_gain_grad = jnp.concatenate([lax.optimization_barrier(jnp.sum(grad_qn * query_hat, axis=(0, 1))), lax.optimization_barrier(jnp.sum(key_normed_gradient * key_unit_normed, axis=(0, 1)))])
    query_low = root_mean_square_backward(grad_qn, query_hat, query_scale, query_key_gain[:HEAD_SIZE]).astype(jnp.bfloat16).reshape(TOKEN_TOTAL, QUERY_HEAD_COUNT * HEAD_SIZE)
    key_reduced_precision = root_mean_square_backward(key_normed_gradient, key_unit_normed, key_norm_scale, query_key_gain[HEAD_SIZE:]).astype(jnp.bfloat16).reshape(TOKEN_TOTAL, KEY_VALUE_HEADS * HEAD_SIZE)
    query_grad = jnp.dot(first_hidden_state.T, query_low, preferred_element_type=jnp.float32)
    key_grad = jnp.dot(first_hidden_state.T, key_reduced_precision, preferred_element_type=jnp.float32)
    value_grad = jnp.dot(first_hidden_state.T, gradient_of_value, preferred_element_type=jnp.float32)
    grad_one = jnp.dot(query_low, query_weight.T, preferred_element_type=jnp.float32) + jnp.dot(key_reduced_precision, key_matrix.T, preferred_element_type=jnp.float32) + jnp.dot(gradient_of_value, value_matrix.T, preferred_element_type=jnp.float32)
    attn_gain_grad = lax.optimization_barrier(jnp.sum(grad_one * normed_one, axis=0))
    tokens_grad = grad_mixed_all + root_mean_square_backward(grad_one, normed_one, scale_one, attn_gain)
    return (to_dealt(result_all), to_dealt(tokens_grad), query_grad, key_grad, value_grad, out_grad, gate_grad, up_grad, down_grad, attn_gain_grad, qk_gain_grad, mlp_gain_grad)
```

```python
import math

import jax
import jax.numpy as jnp
from jax import lax
from jax.experimental import pallas as pl
from jax.experimental.pallas import tpu as pltpu
from jax.sharding import PartitionSpec as P

MODEL_WIDTH = 1024
QUERY_HEAD_COUNT = 16
KEY_VALUE_HEADS = 8
HEAD_SIZE = 64
FF = 4608
SEQUENCE_COUNT = 2
DOCUMENT_IDS = 8


eps_norm = 1e-05
rope_base = 1000000.0


def rms_forward(values, gain_vec):
    norm_scale = lax.rsqrt(jnp.mean(values * values, axis=-1, keepdims=True) + eps_norm)
    normed = values * norm_scale
    return (normed, norm_scale, normed * gain_vec)


def root_mean_square_backward(grad_out, normed, norm_scale, gain_vec):
    grad_normed = grad_out * gain_vec
    inner_term = jnp.mean(grad_normed * normed, axis=-1, keepdims=True)
    return norm_scale * (grad_normed - normed * inner_term)


def rope_tables(positions, head_width):
    half_width = head_width // 2
    frequency = rope_base ** (-(jnp.arange(half_width, dtype=jnp.float32) * 2.0) / head_width)
    angles = positions.astype(jnp.float32)[:, None] * frequency[None, :]
    return (jnp.cos(angles), jnp.sin(angles))


def apply_rotary(values, cosine_table, sine_table, direction):
    half_width = values.shape[-1] // 2
    first_half = values[..., :half_width]
    second_half = values[..., half_width:]
    cos_part = cosine_table[:, None, :]
    sin_part = sine_table[:, None, :] * direction
    return jnp.concatenate(
        [
            first_half * cos_part - second_half * sin_part,
            second_half * cos_part + first_half * sin_part,
        ],
        axis=-1,
    )


def local(
    tokens,
    block_order,
    segment_ids,
    attn_gain,
    query_weight,
    key_matrix,
    value_matrix,
    query_key_gain,
    out_weight,
    mlp_gain,
    gate_weight,
    up_weight,
    down_weight,
    cotangent,
):
    ctx_count = lax.axis_size("ctx")
    sharded_weight_count = lax.axis_size("wsh")
    ctx_index = lax.axis_index("ctx")
    wsh_index = lax.axis_index("wsh")
    row_number = tokens.shape[0]
    ctx_rows = row_number * sharded_weight_count
    half_rows = ctx_rows // SEQUENCE_COUNT
    total_tokens = segment_ids.shape[0]
    block_len = total_tokens // block_order.shape[0]
    seq_len = total_tokens // SEQUENCE_COUNT
    local_heads = QUERY_HEAD_COUNT // sharded_weight_count
    device_local_groups = KEY_VALUE_HEADS // sharded_weight_count
    repeat_heads = QUERY_HEAD_COUNT // KEY_VALUE_HEADS
    score_scale = HEAD_SIZE ** (-0.5)
    span_width = FF // (ctx_count * sharded_weight_count)
    token_ids = (
        block_order[:, None] * block_len + jnp.arange(block_len, dtype=jnp.int32)[None, :]
    ).reshape(-1)
    own_ids = lax.dynamic_slice_in_dim(
        token_ids, (ctx_index * sharded_weight_count + wsh_index) * row_number, row_number
    )
    cosine_table, sine_table = rope_tables(own_ids % seq_len, HEAD_SIZE)
    full_query, full_key, full_value, full_out = (
        lax.all_gather(query_weight, "wsh", axis=0, tiled=True),
        lax.all_gather(key_matrix, "wsh", axis=0, tiled=True),
        lax.all_gather(value_matrix, "wsh", axis=0, tiled=True),
        lax.all_gather(out_weight, "wsh", axis=0, tiled=True),
    )
    gate_parts = jnp.swapaxes(
        gate_weight.reshape(-1, ctx_count, sharded_weight_count, span_width), 1, 2
    )
    up_parts = jnp.swapaxes(
        up_weight.reshape(-1, ctx_count, sharded_weight_count, span_width), 1, 2
    )
    down_parts = down_weight.reshape(
        ctx_count // sharded_weight_count, sharded_weight_count, span_width, MODEL_WIDTH
    )
    gate_cols, up_cols, down_cols = (
        lax.all_to_all(gate_parts, "wsh", split_axis=1, concat_axis=0, tiled=True),
        lax.all_to_all(up_parts, "wsh", split_axis=1, concat_axis=0, tiled=True),
        lax.all_to_all(down_parts, "wsh", split_axis=1, concat_axis=0, tiled=True),
    )
    gate_local = gate_cols.reshape(MODEL_WIDTH, -1)
    up_local = up_cols.reshape(MODEL_WIDTH, -1)
    down_local = down_cols.reshape(-1, MODEL_WIDTH)
    inputs = tokens.astype(jnp.float32)
    normed_one, scale_one, pre_one = rms_forward(inputs, attn_gain)
    first_hidden_state = pre_one.astype(jnp.bfloat16)
    query_pre = jnp.dot(first_hidden_state, full_query, preferred_element_type=jnp.float32).reshape(
        row_number, QUERY_HEAD_COUNT, HEAD_SIZE
    )
    key_before_norm = jnp.dot(
        first_hidden_state, full_key, preferred_element_type=jnp.float32
    ).reshape(row_number, KEY_VALUE_HEADS, HEAD_SIZE)
    value_reduced_precision = jnp.dot(
        first_hidden_state, full_value, preferred_element_type=jnp.float32
    ).astype(jnp.bfloat16)
    query_hat, query_scale, query_normed = rms_forward(query_pre, query_key_gain[:HEAD_SIZE])
    key_unit_normed, key_norm_scale, key_normed = rms_forward(
        key_before_norm, query_key_gain[HEAD_SIZE:]
    )
    query_rotary = (
        apply_rotary(query_normed, cosine_table, sine_table, 1.0)
        .astype(jnp.bfloat16)
        .reshape(row_number, QUERY_HEAD_COUNT * HEAD_SIZE)
    )
    key_rotary = (
        apply_rotary(key_normed, cosine_table, sine_table, 1.0)
        .astype(jnp.bfloat16)
        .reshape(row_number, KEY_VALUE_HEADS * HEAD_SIZE)
    )
    query_heads, key_heads, value_heads = (
        lax.all_to_all(query_rotary, "wsh", split_axis=1, concat_axis=0, tiled=True),
        lax.all_to_all(key_rotary, "wsh", split_axis=1, concat_axis=0, tiled=True),
        lax.all_to_all(value_reduced_precision, "wsh", split_axis=1, concat_axis=0, tiled=True),
    )
    key_every, value_every = (
        lax.all_gather(key_heads, "ctx", axis=0, tiled=True),
        lax.all_gather(value_heads, "ctx", axis=0, tiled=True),
    )
    group_size = math.gcd(ctx_count, max(1, 1024 // half_rows))
    group_count = ctx_count // group_size
    key_groups = key_every.reshape(
        group_count, group_size, SEQUENCE_COUNT, half_rows, device_local_groups, HEAD_SIZE
    )
    value_groups = value_every.reshape(
        group_count, group_size, SEQUENCE_COUNT, half_rows, device_local_groups, HEAD_SIZE
    )
    id_groups = token_ids.reshape(group_count, group_size, SEQUENCE_COUNT, half_rows)
    seg_groups = segment_ids[token_ids].reshape(group_count, group_size, SEQUENCE_COUNT, half_rows)
    ctx_ids = lax.dynamic_slice_in_dim(token_ids, ctx_index * ctx_rows, ctx_rows).reshape(
        SEQUENCE_COUNT, half_rows
    )
    ctx_segs = segment_ids[ctx_ids]
    query_rows = query_heads.reshape(
        SEQUENCE_COUNT, half_rows, device_local_groups, repeat_heads, HEAD_SIZE
    )

    def seq_major(group_piece):
        return jnp.swapaxes(group_piece, 0, 1).reshape(
            (SEQUENCE_COUNT, group_size * half_rows) + group_piece.shape[3:]
        )

    def score_block(key_piece, id_piece, seg_piece):
        keys_seq = seq_major(key_piece)
        ids_seq = seq_major(id_piece)
        segs_seq = seq_major(seg_piece)
        scores = (
            jnp.einsum(
                "sqgrd,skgd->sgrqk", query_rows, keys_seq, preferred_element_type=jnp.float32
            )
            * score_scale
        )
        allowed = (segs_seq[:, None, :] == ctx_segs[:, :, None]) & (
            ids_seq[:, None, :] <= ctx_ids[:, :, None]
        )
        return (scores, allowed[:, None, None], keys_seq)

    def max_step(state_now, pieces):
        run_max, run_sum = state_now
        scores, allowed, unused = score_block(pieces[0], pieces[1], pieces[2])
        masked = jnp.where(allowed, scores, -1e30)
        new_max = jnp.maximum(run_max, jnp.max(masked, axis=-1))
        weights_now = jnp.where(allowed, jnp.exp(masked - new_max[..., None]), 0.0)
        run_sum = run_sum * jnp.exp(run_max - new_max) + jnp.sum(weights_now, axis=-1)
        return ((new_max, run_sum), None)

    stat_shape = (SEQUENCE_COUNT, device_local_groups, repeat_heads, half_rows)
    stats, unused_out = lax.scan(
        max_step,
        (jnp.full(stat_shape, -1e30, jnp.float32), jnp.zeros(stat_shape, jnp.float32)),
        (key_groups, id_groups, seg_groups),
    )
    log_total = stats[0] + jnp.log(stats[1])

    def out_step(running, pieces):
        scores, allowed, unused = score_block(pieces[0], pieces[2], pieces[3])
        prob_low = jnp.where(allowed, jnp.exp(scores - log_total[..., None]), 0.0).astype(
            jnp.bfloat16
        )
        values_seq = seq_major(pieces[1])
        return (
            running
            + jnp.einsum(
                "sgrqk,skgd->sqgrd", prob_low, values_seq, preferred_element_type=jnp.float32
            ),
            None,
        )

    attended, unused_out = lax.scan(
        out_step,
        jnp.zeros(
            (SEQUENCE_COUNT, half_rows, device_local_groups, repeat_heads, HEAD_SIZE), jnp.float32
        ),
        (key_groups, value_groups, id_groups, seg_groups),
    )
    attended_low = attended.astype(jnp.bfloat16)
    attn_tokens = lax.all_to_all(
        attended_low.reshape(ctx_rows, local_heads * HEAD_SIZE),
        "wsh",
        split_axis=0,
        concat_axis=1,
        tiled=True,
    )
    mixed = inputs + jnp.dot(attn_tokens, full_out, preferred_element_type=jnp.float32)
    normed_two, scale_two, pre_two = rms_forward(mixed, mlp_gain)
    hidden_two = pre_two.astype(jnp.bfloat16)
    rows_every, target_every = (
        lax.all_gather(hidden_two, "wsh", axis=0, tiled=True),
        lax.all_gather(cotangent, "wsh", axis=0, tiled=True),
    )
    gate_pre = jnp.dot(rows_every, gate_local, preferred_element_type=jnp.float32)
    up_pre = jnp.dot(rows_every, up_local, preferred_element_type=jnp.float32)
    sigmoid_gate = jax.nn.sigmoid(gate_pre)
    swished = gate_pre * sigmoid_gate
    inner_low = (swished * up_pre).astype(jnp.bfloat16)
    output = (
        mixed
        + lax.psum_scatter(
            jnp.dot(inner_low, down_local, preferred_element_type=jnp.float32).astype(jnp.bfloat16),
            "wsh",
            scatter_dimension=0,
            tiled=True,
        ).astype(jnp.float32)
    ).astype(jnp.bfloat16)
    down_part = jnp.dot(inner_low.T, target_every, preferred_element_type=jnp.float32)
    grad_inner = jnp.dot(target_every, down_local.T, preferred_element_type=jnp.float32)
    gate_low = (
        grad_inner * up_pre * sigmoid_gate * (1.0 + gate_pre * (1.0 - sigmoid_gate))
    ).astype(jnp.bfloat16)
    up_low = (grad_inner * swished).astype(jnp.bfloat16)
    gate_part = jnp.dot(rows_every.T, gate_low, preferred_element_type=jnp.float32)
    up_part = jnp.dot(rows_every.T, up_low, preferred_element_type=jnp.float32)
    grad_two = lax.psum_scatter(
        (
            jnp.dot(gate_low, gate_local.T, preferred_element_type=jnp.float32)
            + jnp.dot(up_low, up_local.T, preferred_element_type=jnp.float32)
        ).astype(jnp.bfloat16),
        "wsh",
        scatter_dimension=0,
        tiled=True,
    ).astype(jnp.float32)
    gate_ctx, up_ctx, down_done = (
        lax.psum_scatter(
            gate_part.astype(jnp.bfloat16), "ctx", scatter_dimension=0, tiled=True
        ).astype(jnp.float32),
        lax.psum_scatter(
            up_part.astype(jnp.bfloat16), "ctx", scatter_dimension=0, tiled=True
        ).astype(jnp.float32),
        lax.psum_scatter(
            down_part.astype(jnp.bfloat16), "ctx", scatter_dimension=0, tiled=True
        ).astype(jnp.float32),
    )
    mlp_gain_grad = jnp.sum(grad_two * normed_two, axis=0)
    grad_mixed = cotangent.astype(jnp.float32) + root_mean_square_backward(
        grad_two, normed_two, scale_two, mlp_gain
    )
    mixed_low = grad_mixed.astype(jnp.bfloat16)
    out_grad = jnp.dot(attn_tokens.T, mixed_low, preferred_element_type=jnp.float32)
    dout_low = jnp.dot(mixed_low, full_out.T, preferred_element_type=jnp.float32).astype(
        jnp.bfloat16
    )
    dout_heads = lax.all_to_all(dout_low, "wsh", split_axis=1, concat_axis=0, tiled=True)
    dout_q = dout_heads.reshape(
        SEQUENCE_COUNT, half_rows, device_local_groups, repeat_heads, HEAD_SIZE
    )
    row_delta = jnp.sum(
        dout_q.astype(jnp.float32) * attended_low.astype(jnp.float32), axis=-1
    ).transpose(0, 2, 3, 1)

    def grad_step(query_acc, pieces):
        scores, allowed, keys_seq = score_block(pieces[0], pieces[2], pieces[3])
        values_seq = seq_major(pieces[1])
        prob_full = jnp.where(allowed, jnp.exp(scores - log_total[..., None]), 0.0)
        prob_low = prob_full.astype(jnp.bfloat16)
        value_part = jnp.einsum(
            "sgrqk,sqgrd->skgd", prob_low, dout_q, preferred_element_type=jnp.float32
        )
        grad_prob = jnp.einsum(
            "sqgrd,skgd->sgrqk", dout_q, values_seq, preferred_element_type=jnp.float32
        )
        score_low = (prob_full * (grad_prob - row_delta[..., None]) * score_scale).astype(
            jnp.bfloat16
        )
        query_acc = query_acc + jnp.einsum(
            "sgrqk,skgd->sqgrd", score_low, keys_seq, preferred_element_type=jnp.float32
        )
        key_part = jnp.einsum(
            "sgrqk,sqgrd->skgd", score_low, query_rows, preferred_element_type=jnp.float32
        )
        return (query_acc, (key_part, value_part))

    query_rows_gradient, kv_parts = lax.scan(
        grad_step,
        jnp.zeros(
            (SEQUENCE_COUNT, half_rows, device_local_groups, repeat_heads, HEAD_SIZE), jnp.float32
        ),
        (key_groups, value_groups, id_groups, seg_groups),
    )

    def to_gathered(stacked):
        shaped = stacked.reshape(
            group_count, SEQUENCE_COUNT, group_size, half_rows, device_local_groups * HEAD_SIZE
        )
        return jnp.swapaxes(shaped, 1, 2).reshape(
            ctx_count * ctx_rows, device_local_groups * HEAD_SIZE
        )

    key_sums, value_sums = (
        lax.psum_scatter(
            to_gathered(kv_parts[0]).astype(jnp.bfloat16), "ctx", scatter_dimension=0, tiled=True
        ).astype(jnp.float32),
        lax.psum_scatter(
            to_gathered(kv_parts[1]).astype(jnp.bfloat16), "ctx", scatter_dimension=0, tiled=True
        ).astype(jnp.float32),
    )
    query_tok, key_token_rows, value_tok, gate_mixed, up_mixed = (
        lax.all_to_all(
            query_rows_gradient.reshape(ctx_rows, local_heads * HEAD_SIZE).astype(jnp.bfloat16),
            "wsh",
            split_axis=0,
            concat_axis=1,
            tiled=True,
        ).astype(jnp.float32),
        lax.all_to_all(
            key_sums.astype(jnp.bfloat16), "wsh", split_axis=0, concat_axis=1, tiled=True
        ).astype(key_sums.dtype),
        lax.all_to_all(
            value_sums.astype(jnp.bfloat16), "wsh", split_axis=0, concat_axis=1, tiled=True
        ).astype(value_sums.dtype),
        lax.all_to_all(
            gate_ctx.astype(jnp.bfloat16), "wsh", split_axis=0, concat_axis=1, tiled=True
        ).astype(gate_ctx.dtype),
        lax.all_to_all(
            up_ctx.astype(jnp.bfloat16), "wsh", split_axis=0, concat_axis=1, tiled=True
        ).astype(up_ctx.dtype),
    )

    def column_order(matrix):
        return jnp.swapaxes(
            matrix.reshape(matrix.shape[0], sharded_weight_count, ctx_count, span_width), 1, 2
        ).reshape(matrix.shape[0], FF)

    gate_done = column_order(gate_mixed)
    up_done = column_order(up_mixed)
    grad_qn = apply_rotary(
        query_tok.reshape(row_number, QUERY_HEAD_COUNT, HEAD_SIZE), cosine_table, sine_table, -1.0
    )
    key_normed_gradient = apply_rotary(
        key_token_rows.reshape(row_number, KEY_VALUE_HEADS, HEAD_SIZE),
        cosine_table,
        sine_table,
        -1.0,
    )
    qk_gain_grad = jnp.concatenate(
        [
            jnp.sum(grad_qn * query_hat, axis=(0, 1)),
            jnp.sum(key_normed_gradient * key_unit_normed, axis=(0, 1)),
        ]
    )
    query_low = (
        root_mean_square_backward(grad_qn, query_hat, query_scale, query_key_gain[:HEAD_SIZE])
        .astype(jnp.bfloat16)
        .reshape(row_number, QUERY_HEAD_COUNT * HEAD_SIZE)
    )
    key_reduced_precision = (
        root_mean_square_backward(
            key_normed_gradient, key_unit_normed, key_norm_scale, query_key_gain[HEAD_SIZE:]
        )
        .astype(jnp.bfloat16)
        .reshape(row_number, KEY_VALUE_HEADS * HEAD_SIZE)
    )
    value_grad_low = value_tok.astype(jnp.bfloat16)
    query_grad = jnp.dot(first_hidden_state.T, query_low, preferred_element_type=jnp.float32)
    key_grad = jnp.dot(
        first_hidden_state.T, key_reduced_precision, preferred_element_type=jnp.float32
    )
    value_grad = jnp.dot(first_hidden_state.T, value_grad_low, preferred_element_type=jnp.float32)
    grad_one = (
        jnp.dot(query_low, full_query.T, preferred_element_type=jnp.float32)
        + jnp.dot(key_reduced_precision, full_key.T, preferred_element_type=jnp.float32)
        + jnp.dot(value_grad_low, full_value.T, preferred_element_type=jnp.float32)
    )
    attn_gain_grad = jnp.sum(grad_one * normed_one, axis=0)
    tokens_grad = grad_mixed + root_mean_square_backward(grad_one, normed_one, scale_one, attn_gain)
    query_done, key_done, value_done, out_done, attn_gain_done, qk_gain_done, mlp_gain_done = (
        lax.psum_scatter(query_grad, ("ctx", "wsh"), scatter_dimension=0, tiled=True),
        lax.psum_scatter(key_grad, ("ctx", "wsh"), scatter_dimension=0, tiled=True),
        lax.psum_scatter(value_grad, ("ctx", "wsh"), scatter_dimension=0, tiled=True),
        lax.psum_scatter(out_grad, ("ctx", "wsh"), scatter_dimension=0, tiled=True),
        lax.psum_scatter(attn_gain_grad, ("ctx", "wsh"), scatter_dimension=0, tiled=True),
        lax.psum_scatter(qk_gain_grad, ("ctx", "wsh"), scatter_dimension=0, tiled=True),
        lax.psum_scatter(mlp_gain_grad, ("ctx", "wsh"), scatter_dimension=0, tiled=True),
    )
    return (
        output,
        tokens_grad,
        query_done,
        key_done,
        value_done,
        out_done,
        gate_done,
        up_done,
        down_done,
        attn_gain_done,
        qk_gain_done,
        mlp_gain_done,
    )


f32 = jnp.float32
bf16 = jnp.bfloat16
QTILE = 256
KTILE = 256


def heads_fit(mesh):
    ctx_count, wsh_count = mesh.shape["ctx"], mesh.shape["wsh"]
    return wsh_count == 4 and ctx_count == SEQUENCE_COUNT * (QUERY_HEAD_COUNT // wsh_count)


def dot(a, b, dims):
    return lax.dot_general(a, b, (dims, ((), ())), preferred_element_type=f32)


def swap_with(values, axis, distance):
    count = lax.axis_size(axis)
    return lax.ppermute(values, axis, [(i, i ^ distance) for i in range(count)])


def piece(stacked, index, axis=0):
    return lax.dynamic_index_in_dim(stacked, index, axis, keepdims=False)


def gather_wsh(shard):
    own = lax.axis_index("wsh")
    far = swap_with(shard, "wsh", 2)
    near = swap_with(shard, "wsh", 1)
    corner = swap_with(far, "wsh", 1)
    full = jnp.zeros((4,) + shard.shape, shard.dtype)
    for distance, part in ((0, shard), (1, near), (2, far), (3, corner)):
        full = lax.dynamic_update_index_in_dim(full, part, own ^ distance, 0)
    return full.reshape((4 * shard.shape[0],) + shard.shape[1:])


def scatter_sum_wsh(partial):
    own = lax.axis_index("wsh")
    rows = partial.reshape((4, partial.shape[0] // 4) + partial.shape[1:])
    low = rows.astype(bf16)
    send = jnp.stack([piece(low, own ^ 1), piece(low, own ^ 3)])
    near = swap_with(send, "wsh", 1).astype(f32)
    other = (piece(rows, own ^ 2).astype(f32) + near[1]).astype(bf16)
    far = swap_with(other, "wsh", 2).astype(f32)
    return piece(rows, own).astype(f32) + near[0] + far


def scatter_sum_ctx(chunks, bits):
    own = lax.axis_index("ctx")
    left = list(range(len(bits)))[::-1]
    now = chunks.reshape((2,) * len(bits) + chunks.shape[1:])
    for bit in bits:
        axis = left.index(bit)
        left.remove(bit)
        mine = (own >> bit) & 1
        moved = swap_with(piece(now, 1 - mine, axis), "ctx", 1 << bit)
        now = (piece(now, mine, axis).astype(f32) + moved.astype(f32)).astype(bf16)
    return now


def exchange(values, axis):
    return lax.all_to_all(values, axis, split_axis=0, concat_axis=0, tiled=True)


def into_order(order_ref, source_ref, first, target_ref, block_len):
    holders = source_ref.shape[0]
    per_holder = source_ref.shape[2] // block_len
    for holder in range(holders):
        for place in range(per_holder):
            start = pl.multiple_of(order_ref[holder * per_holder + place] * block_len, block_len)
            target_ref[:, pl.ds(start, block_len)] = source_ref[
                holder, first : first + HEAD_SIZE, place * block_len : (place + 1) * block_len
            ]


def out_of_order(order_ref, source_ref, target_ref, first, block_len):
    holders = target_ref.shape[0]
    per_holder = target_ref.shape[2] // block_len
    for holder in range(holders):
        for place in range(per_holder):
            start = pl.multiple_of(order_ref[holder * per_holder + place] * block_len, block_len)
            target_ref[
                holder, first : first + HEAD_SIZE, place * block_len : (place + 1) * block_len
            ] = source_ref[:, pl.ds(start, block_len)].astype(target_ref.dtype)


def allowed_tile(start_row, query_first, key_first):
    key_pos = key_first + lax.broadcasted_iota(jnp.int32, (KTILE, QTILE), 0)
    query_pos = query_first + lax.broadcasted_iota(jnp.int32, (KTILE, QTILE), 1)
    return (key_pos >= start_row) & (key_pos <= query_pos)


def attend_kernel(block_len, order_ref, low_ref, start_ref, qkv_ref, out_ref, lse_ref, q, k, v, o):
    scale = HEAD_SIZE ** (-0.5)
    into_order(order_ref, qkv_ref, 0, q, block_len)
    into_order(order_ref, qkv_ref, HEAD_SIZE, k, block_len)
    into_order(order_ref, qkv_ref, 2 * HEAD_SIZE, v, block_len)
    for tile in range(q.shape[1] // QTILE):
        first = tile * QTILE
        cols = slice(first, first + QTILE)
        q_tile = q[:, cols]
        start_row = start_ref[:, cols]

        def step(j, state):
            total, acc = state
            at = pl.multiple_of(j * KTILE, KTILE)
            scores = dot(k[:, pl.ds(at, KTILE)], q_tile, ((0,), (0,)))
            weights = jnp.where(allowed_tile(start_row, first, at), jnp.exp(scores * scale), 0.0)
            total = total + jnp.sum(weights, axis=0, keepdims=True)
            acc = acc + dot(v[:, pl.ds(at, KTILE)], weights.astype(bf16), ((1,), (0,)))
            return (total, acc)

        total, acc = lax.fori_loop(
            low_ref[tile],
            (first + QTILE - 1) // KTILE + 1,
            step,
            (jnp.zeros((1, QTILE), f32), jnp.zeros((HEAD_SIZE, QTILE), f32)),
        )
        o[:, cols] = (acc / total).astype(bf16)
        lse_ref[:, cols] = jnp.log(total)
    out_of_order(order_ref, o, out_ref, 0, block_len)


def attend_back_kernel(
    block_len, order_ref, low_ref, start_ref, lse_ref, qkv_ref, out_ref, dout_ref, grad_ref,
    q, k, v, o, do, dq, dk, dv,
):
    scale = HEAD_SIZE ** (-0.5)
    into_order(order_ref, qkv_ref, 0, q, block_len)
    into_order(order_ref, qkv_ref, HEAD_SIZE, k, block_len)
    into_order(order_ref, qkv_ref, 2 * HEAD_SIZE, v, block_len)
    into_order(order_ref, out_ref, 0, o, block_len)
    into_order(order_ref, dout_ref, 0, do, block_len)
    dk[...] = jnp.zeros(dk.shape, f32)
    dv[...] = jnp.zeros(dv.shape, f32)
    for tile in range(q.shape[1] // QTILE):
        first = tile * QTILE
        cols = slice(first, first + QTILE)
        q_tile = q[:, cols]
        do_tile = do[:, cols]
        start_row = start_ref[:, cols]
        lse_row = lse_ref[:, cols]
        delta = jnp.sum(do_tile.astype(f32) * o[:, cols].astype(f32), axis=0, keepdims=True)

        def step(j, acc):
            at = pl.multiple_of(j * KTILE, KTILE)
            keys = pl.ds(at, KTILE)
            scores = dot(k[:, keys], q_tile, ((0,), (0,)))
            probs = jnp.where(
                allowed_tile(start_row, first, at), jnp.exp(scores * scale - lse_row), 0.0
            )
            grad_probs = dot(v[:, keys], do_tile, ((0,), (0,)))
            dv[:, keys] += dot(do_tile, probs.astype(bf16), ((1,), (1,)))
            grad_scores = (probs * (grad_probs - delta) * scale).astype(bf16)
            dk[:, keys] += dot(q_tile, grad_scores, ((1,), (1,)))
            return acc + dot(k[:, keys], grad_scores, ((1,), (0,)))

        dq[:, cols] = lax.fori_loop(
            low_ref[tile],
            (first + QTILE - 1) // KTILE + 1,
            step,
            jnp.zeros((HEAD_SIZE, QTILE), f32),
        )
    out_of_order(order_ref, dq, grad_ref, 0, block_len)
    out_of_order(order_ref, dk, grad_ref, HEAD_SIZE, block_len)
    out_of_order(order_ref, dv, grad_ref, 2 * HEAD_SIZE, block_len)


def vmem_call(kernel, name, smem_count, vmem_count, out_shape, scratch, flops):
    smem = pl.BlockSpec(memory_space=pltpu.SMEM)
    vmem = pl.BlockSpec(memory_space=pltpu.VMEM)
    return pl.pallas_call(
        kernel,
        name=name,
        in_specs=[smem] * smem_count + [vmem] * vmem_count,
        out_specs=jax.tree.map(lambda unused: vmem, out_shape),
        out_shape=out_shape,
        scratch_shapes=scratch,
        cost_estimate=pl.CostEstimate(flops=flops, transcendentals=0, bytes_accessed=4 << 20),
    )


def rms_heads(values, gain):
    scale = lax.rsqrt(jnp.mean(values * values, axis=1, keepdims=True) + eps_norm)
    hat = values * scale
    return hat, scale, hat * gain[None, :, None]


def rms_heads_back(grad, hat, scale, gain):
    scaled = grad * gain[None, :, None]
    return scale * (scaled - hat * jnp.mean(scaled * hat, axis=1, keepdims=True))


def turn(values, cosine, sine):
    half = values.shape[1] // 2
    a, b = values[:, :half], values[:, half:]
    return jnp.concatenate([a * cosine - b * sine, b * cosine + a * sine], axis=1)


def local_heads_apart(
    tokens,
    block_order,
    segment_ids,
    attn_gain,
    query_weight,
    key_matrix,
    value_matrix,
    query_key_gain,
    out_weight,
    mlp_gain,
    gate_weight,
    up_weight,
    down_weight,
    cotangent,
):
    ctx_count = lax.axis_size("ctx")
    wsh_count = lax.axis_size("wsh")
    ctx_index = lax.axis_index("ctx")
    wsh_index = lax.axis_index("wsh")
    own_rows = tokens.shape[0]
    ctx_rows = own_rows * wsh_count
    half_rows = ctx_rows // SEQUENCE_COUNT
    token_total = segment_ids.shape[0]
    block_len = token_total // block_order.shape[0]
    seq_len = token_total // SEQUENCE_COUNT
    seq_blocks = seq_len // block_len
    heads = QUERY_HEAD_COUNT // wsh_count
    groups = KEY_VALUE_HEADS // wsh_count
    repeat = heads // groups
    q_width, kv_width = heads * HEAD_SIZE, groups * HEAD_SIZE
    qkv_width = q_width + 2 * kv_width
    hidden = FF // wsh_count
    ctx_bits = ctx_count.bit_length() - 1
    up_bits = list(range(ctx_bits))
    turned_bits = up_bits[1:] + up_bits[:1]

    tokens_ctx = gather_wsh(tokens)
    qkv_parts = jnp.concatenate(
        [
            query_weight.reshape(-1, wsh_count, q_width),
            key_matrix.reshape(-1, wsh_count, kv_width),
            value_matrix.reshape(-1, wsh_count, kv_width),
        ],
        axis=2,
    )
    qkv_weight = exchange(jnp.swapaxes(qkv_parts, 0, 1), "wsh").reshape(MODEL_WIDTH, qkv_width)
    gate_weight, up_weight, out_shard, cot_shard, tokens_ctx, qkv_weight = lax.optimization_barrier(
        (gate_weight, up_weight, out_weight, cotangent, tokens_ctx, qkv_weight)
    )
    full_out = gather_wsh(out_shard)

    def hidden_columns(weight):
        parts = jnp.swapaxes(weight.reshape(-1, wsh_count, hidden), 0, 1)
        return exchange(parts, "wsh").reshape(MODEL_WIDTH, hidden)

    gate_local = hidden_columns(gate_weight)
    up_local = hidden_columns(up_weight)
    cot_ctx = gather_wsh(cot_shard)

    blocks = lax.dynamic_slice_in_dim(block_order, ctx_index * wsh_count, wsh_count)
    positions = (blocks[:, None] * block_len + jnp.arange(block_len)[None, :]).reshape(-1) % seq_len
    cosine, sine = rope_tables(positions, HEAD_SIZE)
    cosine, sine = cosine.T[None], sine.T[None]
    own_seq = ctx_index // heads
    order_all = block_order.reshape(ctx_count, SEQUENCE_COUNT, -1) % seq_blocks
    order = piece(order_all, own_seq, 1).reshape(-1)
    seq_segs = lax.dynamic_slice_in_dim(segment_ids, own_seq * seq_len, seq_len)
    before = jnp.sum(
        seq_segs[None, :] < jnp.arange(DOCUMENT_IDS)[:, None], axis=1, dtype=jnp.int32
    )
    doc_start = jnp.sum(
        jnp.where(seq_segs[None, :] == jnp.arange(DOCUMENT_IDS)[:, None], before[:, None], 0), axis=0
    )
    low_tile = doc_start[::QTILE] // KTILE
    start_row = doc_start[None, :]

    inputs = tokens_ctx.astype(f32)
    normed_one, scale_one, pre_one = rms_forward(inputs, attn_gain)
    hidden_one = pre_one.astype(bf16)
    qkv_pre = dot(qkv_weight, hidden_one, ((0,), (1,)))
    q_gain, k_gain = query_key_gain[:HEAD_SIZE], query_key_gain[HEAD_SIZE:]
    q_hat, q_scale, q_normed = rms_heads(qkv_pre[:q_width].reshape(heads, HEAD_SIZE, -1), q_gain)
    k_hat, k_scale, k_normed = rms_heads(
        qkv_pre[q_width : q_width + kv_width].reshape(groups, HEAD_SIZE, -1), k_gain
    )
    q_low = turn(q_normed, cosine, sine).astype(bf16)
    k_low = turn(k_normed, cosine, sine).astype(bf16)
    v_low = qkv_pre[q_width + kv_width :].reshape(groups, HEAD_SIZE, -1).astype(bf16)

    def to_heads(features):
        split = features.reshape(heads, -1, SEQUENCE_COUNT, half_rows)
        return split.transpose(2, 0, 1, 3).reshape(ctx_count, -1, half_rows)

    def from_heads(received):
        split = received.reshape(SEQUENCE_COUNT, heads, -1, half_rows)
        return split.transpose(1, 2, 0, 3).reshape(heads, -1, ctx_rows)

    qkv_low = jnp.concatenate(
        [q_low, jnp.repeat(k_low, repeat, axis=0), jnp.repeat(v_low, repeat, axis=0)], axis=1
    )
    qkv_head = exchange(to_heads(qkv_low), "ctx")
    tile_flops = 2 * seq_len * seq_len * HEAD_SIZE
    low_seq = pltpu.VMEM((HEAD_SIZE, seq_len), bf16)
    wide_seq = pltpu.VMEM((HEAD_SIZE, seq_len), f32)
    out_head, lse = vmem_call(
        lambda *refs: attend_kernel(block_len, *refs),
        "attend",
        2,
        2,
        [
            jax.ShapeDtypeStruct((ctx_count, HEAD_SIZE, half_rows), bf16),
            jax.ShapeDtypeStruct((1, seq_len), f32),
        ],
        [low_seq] * 4,
        tile_flops,
    )(order, low_tile, start_row, qkv_head)
    attn_local = from_heads(exchange(out_head, "ctx")).reshape(q_width, ctx_rows)
    attn_full = gather_wsh(attn_local)

    mixed = inputs + dot(attn_full, full_out, ((0,), (0,)))
    normed_two, scale_two, pre_two = rms_forward(mixed, mlp_gain)
    hidden_two = pre_two.astype(bf16)
    gate_pre = dot(hidden_two, gate_local, ((1,), (0,)))
    up_pre = dot(hidden_two, up_local, ((1,), (0,)))
    sigmoid_gate = jax.nn.sigmoid(gate_pre)
    swished = gate_pre * sigmoid_gate
    inner_low = (swished * up_pre).astype(bf16)
    grad_inner = dot(cot_ctx, down_weight, ((1,), (1,)))
    gate_low = (
        grad_inner * up_pre * sigmoid_gate * (1.0 + gate_pre * (1.0 - sigmoid_gate))
    ).astype(bf16)
    up_low = (grad_inner * swished).astype(bf16)
    grad_two = scatter_sum_wsh(
        dot(gate_low, gate_local, ((1,), (1,))) + dot(up_low, up_local, ((1,), (1,)))
    )

    def own(rows):
        return lax.dynamic_slice_in_dim(rows, wsh_index * own_rows, own_rows)

    normed_two_own = own(normed_two)
    mlp_gain_part = jnp.sum(grad_two * normed_two_own, axis=0)
    grad_mixed = cotangent.astype(f32) + root_mean_square_backward(
        grad_two, normed_two_own, own(scale_two), mlp_gain
    )
    mixed_low = gather_wsh(grad_mixed.astype(bf16))

    def down_chunks(part):
        return part.astype(bf16).reshape(ctx_count, -1, part.shape[-1])

    gate_part = down_chunks(dot(hidden_two, gate_low, ((0,), (0,))))
    up_part = down_chunks(dot(hidden_two, up_low, ((0,), (0,))))
    down_part = down_chunks(dot(inner_low, cot_ctx, ((0,), (0,))))
    gate_sum = scatter_sum_ctx(gate_part, up_bits)
    up_sum = scatter_sum_ctx(up_part, turned_bits)
    half_width = MODEL_WIDTH // 2
    down_sum = jnp.concatenate(
        [
            scatter_sum_ctx(down_part[:, :, :half_width], up_bits),
            scatter_sum_ctx(down_part[:, :, half_width:], turned_bits),
        ],
        axis=1,
    )
    output = (
        own(mixed) + scatter_sum_wsh(dot(inner_low, down_weight, ((1,), (0,))))
    ).astype(bf16)

    dout_local = dot(out_weight, mixed_low, ((1,), (1,))).astype(bf16)
    dout_head = exchange(to_heads(dout_local), "ctx")
    grad_head = vmem_call(
        lambda *refs: attend_back_kernel(block_len, *refs),
        "attend_back",
        2,
        5,
        jax.ShapeDtypeStruct((ctx_count, 3 * HEAD_SIZE, half_rows), bf16),
        [low_seq] * 5 + [wide_seq] * 3,
        3 * tile_flops,
    )(order, low_tile, start_row, lse, qkv_head, out_head, dout_head)
    out_part = dot(attn_local, mixed_low, ((1,), (0,)))
    out_sum = scatter_sum_ctx(down_chunks(out_part), turned_bits)
    grads = from_heads(exchange(grad_head, "ctx")).astype(f32)
    grad_q = grads[:, :HEAD_SIZE]
    grad_kv = jnp.sum(grads[:, HEAD_SIZE:].reshape(groups, repeat, 2 * HEAD_SIZE, ctx_rows), axis=1)
    grad_qn = turn(grad_q, cosine, -sine)
    grad_kn = turn(grad_kv[:, :HEAD_SIZE], cosine, -sine)
    qk_gain_part = jnp.concatenate(
        [jnp.sum(grad_qn * q_hat, axis=(0, 2)), jnp.sum(grad_kn * k_hat, axis=(0, 2))]
    )
    qkv_grad_low = jnp.concatenate(
        [
            rms_heads_back(grad_qn, q_hat, q_scale, q_gain).astype(bf16).reshape(q_width, -1),
            rms_heads_back(grad_kn, k_hat, k_scale, k_gain).astype(bf16).reshape(kv_width, -1),
            grad_kv[:, HEAD_SIZE:].astype(bf16).reshape(kv_width, -1),
        ]
    )
    grad_one = scatter_sum_wsh(dot(qkv_grad_low, qkv_weight, ((0,), (1,))))
    qkv_part = down_chunks(dot(hidden_one, qkv_grad_low, ((0,), (1,))))
    qkv_sum = scatter_sum_ctx(qkv_part, up_bits)
    normed_one_own = own(normed_one)
    attn_gain_part = jnp.sum(grad_one * normed_one_own, axis=0)
    tokens_grad = grad_mixed + root_mean_square_backward(
        grad_one, normed_one_own, own(scale_one), attn_gain
    )

    def columns_home(summed):
        rows = exchange(summed.reshape(wsh_count, -1, summed.shape[-1]), "wsh")
        return rows.astype(f32)

    def side_by_side(rows):
        return jnp.swapaxes(rows, 0, 1).reshape(rows.shape[1], -1)

    home = [
        (c * wsh_count + w, w * ctx_count + c)
        for c in range(ctx_count)
        for w in range(wsh_count)
    ]

    def rows_home(summed):
        return lax.ppermute(summed, ("ctx", "wsh"), home).astype(f32)

    gate_done = side_by_side(columns_home(gate_sum))
    up_done = side_by_side(columns_home(up_sum))
    qkv_rows = columns_home(qkv_sum)
    device_count = ctx_count * wsh_count
    gains = jnp.concatenate(
        [
            attn_gain_part.reshape(device_count, -1),
            qk_gain_part.reshape(device_count, -1),
            mlp_gain_part.reshape(device_count, -1),
        ],
        axis=1,
    ).reshape(ctx_count, wsh_count, -1)
    gains = jnp.sum(exchange(jnp.swapaxes(gains, 0, 1), "wsh"), axis=0)
    gains = jnp.sum(exchange(gains, "ctx"), axis=0)
    model_share = MODEL_WIDTH // device_count
    return (
        output,
        tokens_grad,
        side_by_side(qkv_rows[:, :, :q_width]),
        side_by_side(qkv_rows[:, :, q_width : q_width + kv_width]),
        side_by_side(qkv_rows[:, :, q_width + kv_width :]),
        rows_home(out_sum),
        gate_done,
        up_done,
        rows_home(down_sum),
        gains[:model_share],
        gains[model_share:-model_share],
        gains[-model_share:],
    )


def solution(mesh):
    in_specs = (
        P(("ctx", "wsh"), None),
        P(),
        P(),
        P(),
        P("wsh", None),
        P("wsh", None),
        P("wsh", None),
        P(),
        P("wsh", None),
        P(),
        P("wsh", None),
        P("wsh", None),
        P("wsh", None),
        P(("ctx", "wsh"), None),
    )
    out_specs = (
        P(("ctx", "wsh"), None),
        P(("ctx", "wsh"), None),
        P(("ctx", "wsh"), None),
        P(("ctx", "wsh"), None),
        P(("ctx", "wsh"), None),
        P(("ctx", "wsh"), None),
        P(("ctx", "wsh"), None),
        P(("ctx", "wsh"), None),
        P(("ctx", "wsh"), None),
        P(("ctx", "wsh")),
        P(("ctx", "wsh")),
        P(("ctx", "wsh")),
    )
    body = local_heads_apart if heads_fit(mesh) else local
    return jax.shard_map(body, mesh=mesh, in_specs=in_specs, out_specs=out_specs, check_vma=False)
```
